512 devices in a mesh: wide: 64 (over y, z), narrow: 8 (over x, core).
Axes of the slice: x: 4, y: 8, z: 8, core: 2. Of those that a mesh axis runs over, the one named last changes fastest.
Arguments:
- right_side: bfloat16 [4, 1024, 512], P(None, 'wide'), may hold values from -6 to 6
- partial_in: float32 [8, 4, 1024, 512], P('narrow', None, 'wide'), may hold values from -6 to 6
- window_factor: bfloat16 [4, 1024, 4, 1024], P(None, 'wide', None, 'narrow'), may hold values from -0.09375 to 0.09375
- inverse_t: bfloat16 [4, 1024, 1024], P(None, 'wide', 'narrow'), as said below
- trailing_factor: bfloat16 [131072, 4, 1024], P('wide', None, 'narrow'), may hold values from -0.09375 to 0.09375
Outputs:
- solved: bfloat16 [4, 1024, 512], P(None, 'narrow')
- trailing: float32 [131072, 512], P(('wide', 'narrow'))
The draws below stay inside these ranges and needn't reach their ends.
Inputs may be any that keep to these rules, and one draw needn't show every extreme that they name: inverse_t[k] is the transpose of the inverse of the k-th diagonal block of the lower-triangular factor: entry [k, j, i] is zero where j > i.
All inputs are finite; a program needn't handle non-finite values.
Results may differ from the reference program's by a relative error of at most 0.012.
Values may be sent and summed in bfloat16 or wider, within the bound.
No kernel may reach another device: no remote copies, remote signals or barrier semaphores. Data moves between devices by JAX's collectives and lax.ppermute only.
A program may use at most 64 MiB of HBM per device.

```python
import math
import jax
import jax.numpy as jnp

NB = 1024
RHS = 512
STEPS = 4
ROWS = 131072
N_NARROW = 8


def draw_inverse_t(key, part):
    key_off, key_diag = jax.random.split(key)
    first = jnp.arange(NB)[:, None]
    second = jnp.arange(NB)[None, :]
    below = (first < second).astype(jnp.float32)
    eye = (first == second).astype(jnp.float32)
    offdiag = jax.random.truncated_normal(key_off, -4.0, 4.0, (STEPS, NB, NB), jnp.float32)
    diag = jax.random.uniform(key_diag, (STEPS, 1, NB), jnp.float32, 0.5, 1.5)
    values = offdiag * below * (0.5 / math.sqrt(NB)) + diag * eye
    return values.astype(jnp.bfloat16)


def shard_levels(rng, shape, cuts, least, largest):
    gain = 1.0
    for position, shards_of in cuts:
        heights = jax.random.uniform(jax.random.fold_in(jax.random.fold_in(rng, 6), position), (shards_of,), jnp.float32, least / len(cuts), largest / len(cuts))
        gain = gain * jnp.repeat(jnp.exp(heights), shape[position] // shards_of).reshape((-1,) + (1,) * (len(shape) - 1 - position))
    return gain


def centred(stream_key, extent, spread, limit, shards=(), dtype=jnp.bfloat16):
    level = shard_levels(stream_key, extent, shards, -0.22, 0.18) if shards else 1.0
    entries = jax.random.normal(stream_key, extent, jnp.float32) * spread * level
    return jnp.minimum(jnp.maximum(entries, -limit), limit).astype(dtype)


def setup_inputs(seed: int = 0) -> dict:
    streams_of = jax.random.split(jax.random.key(seed), 6)
    right_side = centred(streams_of[0], (STEPS, NB, RHS), 1.0, 6.0, ((1, 64),))
    partial_in = centred(streams_of[1], (N_NARROW, STEPS, NB, RHS), 1.0, 6.0, ((0, 8), (2, 64)), jnp.float32)
    window_factor = centred(streams_of[2], (STEPS, NB, STEPS, NB), (4 * NB) ** -0.5, 0.09375, ((1, 64), (3, 8)))
    inverse_t = draw_inverse_t(jax.random.fold_in(streams_of[5], 71), 0)
    trailing_factor = centred(streams_of[4], (ROWS, STEPS, NB), (STEPS * NB) ** -0.5, 0.09375, ((0, 64), (2, 8)))
    return {"right_side": right_side, "partial_in": partial_in, "window_factor": window_factor, "inverse_t": inverse_t, "trailing_factor": trailing_factor}


def reference(right_side, partial_in, window_factor, inverse_t, trailing_factor):
    solved_list = []
    for block in range(STEPS):
        fanned = jnp.sum(partial_in[:, block], axis=0)
        for prior in range(block):
            fanned = fanned + jnp.dot(window_factor[block, :, prior, :], solved_list[prior], preferred_element_type=jnp.float32)
        residue = (right_side[block].astype(jnp.float32) - fanned).astype(jnp.bfloat16)
        solution = jnp.dot(inverse_t[block].T, residue, preferred_element_type=jnp.float32)
        solved_list.append(solution.astype(jnp.bfloat16))
    solved = jnp.stack(solved_list)
    flat_factor = trailing_factor.reshape(ROWS, STEPS * NB)
    trailing = jnp.dot(flat_factor, solved.reshape(STEPS * NB, RHS), preferred_element_type=jnp.float32)
    return solved, trailing
```

```python
import jax
import jax.numpy as jnp
from jax import lax
from jax.sharding import Mesh
from jax.sharding import PartitionSpec as P

F32 = jnp.float32
BF16 = jnp.bfloat16
NARROW = ("x", "core")
NUM_Y, NUM_Z, NUM_X, NUM_CORE = 8, 8, 4, 2
NUM_NARROW = NUM_X * NUM_CORE


def spread(value, axis, count):
    copies = jnp.broadcast_to(value[None], (count,) + value.shape)
    return lax.all_to_all(copies, axis, 0, 0, tiled=True)


def per_device(right_side, partial_in, window_factor, inverse_t, trailing_factor):
    steps, rows, rhs = right_side.shape
    cols = inverse_t.shape[2]
    part = rhs // NUM_Y
    slab = rows * NUM_Y
    trail_rows = trailing_factor.shape[0]

    first = (lax.axis_index(NARROW) == 0).astype(F32)
    terms = partial_in[0] - right_side.astype(F32) * first
    terms = terms.reshape(steps, rows, NUM_Y, part).transpose(2, 0, 1, 3)
    terms = lax.all_to_all(terms, "y", 0, 0, tiled=True)
    terms = terms.transpose(1, 3, 0, 2).reshape(steps, part, slab)

    pairs = [(block, prior) for block in range(steps) for prior in range(block)]
    pieces = [window_factor[block, :, prior, :] for block, prior in pairs]
    pieces += [inverse_t[block] for block in range(steps)]
    pieces = spread(jnp.stack(pieces), "y", NUM_Y)
    pieces = pieces.transpose(1, 0, 2, 3).reshape(-1, slab, cols)
    window = {pair: pieces[i] for i, pair in enumerate(pairs)}
    inverse = [pieces[len(pairs) + block] for block in range(steps)]

    solved_t = []
    for block in range(steps):
        fanned = terms[block]
        for prior in range(block):
            fanned = fanned + lax.dot_general(
                solved_t[prior], window[block, prior], (((1,), (1,)), ((), ())),
                preferred_element_type=F32,
            )
        fanned = spread(fanned, NARROW, NUM_NARROW).sum(0)
        residue = (-fanned).astype(BF16)
        share = jnp.dot(residue, inverse[block], preferred_element_type=F32)
        share = spread(share, "z", NUM_Z).sum(0)
        solved_t.append(share.astype(BF16))

    every = spread(jnp.stack(solved_t), "y", NUM_Y)
    every = every.transpose(1, 0, 2, 3).reshape(steps, rhs, cols)
    solved = every.transpose(0, 2, 1)

    trailing = jnp.zeros((trail_rows, rhs), F32)
    flat_factor = trailing_factor.reshape(trail_rows, steps * cols)
    flat_solved = solved.reshape(steps * cols, rhs)
    trailing = jnp.dot(flat_factor, flat_solved, preferred_element_type=F32)

    own = trail_rows // NUM_NARROW
    trailing = trailing.reshape(NUM_X, NUM_CORE, own, rhs)
    core = lax.axis_index("core")
    away = lax.dynamic_index_in_dim(trailing, 1 - core, 1, keepdims=False)
    kept = lax.dynamic_index_in_dim(trailing, core, 1, keepdims=False)
    back = lax.ppermute(away.astype(BF16), "core", [(0, 1), (1, 0)])
    pair_sum = (kept + back.astype(F32)).astype(BF16)
    pair_sum = lax.all_to_all(pair_sum, "x", 0, 0, tiled=True)
    trailing = pair_sum.astype(F32).sum(0)
    return (solved, trailing)


def solution(mesh):
    grid = Mesh(
        mesh.devices.reshape(NUM_Y, NUM_Z, NUM_X, NUM_CORE), ("y", "z", "x", "core")
    )
    wide = ("y", "z")
    placed = (
        P(None, wide, None),
        P(NARROW, None, wide, None),
        P(None, wide, None, NARROW),
        P(None, wide, NARROW),
        P(wide, None, NARROW),
    )
    return jax.shard_map(
        per_device,
        mesh=grid,
        in_specs=placed,
        out_specs=(P(None, NARROW, None), P(wide + NARROW, None)),
        check_vma=False,
    )
```

```python
import jax
import jax.numpy as jnp
from jax import lax
from jax.experimental import pallas as pl
from jax.experimental.pallas import tpu as pltpu
from jax.sharding import Mesh
from jax.sharding import PartitionSpec as P

F32 = jnp.float32
BF16 = jnp.bfloat16
NARROW = ("x", "core")
NUM_Y, NUM_Z, NUM_X, NUM_CORE = 8, 8, 4, 2
NUM_NARROW = NUM_X * NUM_CORE


def spread(value, axis, count):
    copies = jnp.broadcast_to(value[None], (count,) + value.shape)
    return lax.all_to_all(copies, axis, 0, 0, tiled=True)


def total(stack):
    return stack.astype(F32).sum(0)


def product(factor, every):
    trail_rows, depth = factor.shape
    groups, steps, part, cols = every.shape
    rhs = groups * part
    own = trail_rows // NUM_NARROW

    def body(core_ref, factor_ref, every_ref, kept_ref, away_ref, flat_ref):
        @pl.when(pl.program_id(0) == 0)
        def _():
            for group in range(groups):
                for step in range(steps):
                    flat_ref[
                        group * part : (group + 1) * part,
                        step * cols : (step + 1) * cols,
                    ] = every_ref[group, step]

        core = core_ref[0]
        terms = (((1,), (1,)), ((), ()))
        kept_ref[0] = lax.dot_general(
            factor_ref[pl.ds(pl.multiple_of(core * own, own), own), :],
            flat_ref[...], terms, preferred_element_type=F32,
        )
        away_ref[0] = lax.dot_general(
            factor_ref[pl.ds(pl.multiple_of((1 - core) * own, own), own), :],
            flat_ref[...], terms, preferred_element_type=F32,
        ).astype(BF16)

    return pl.pallas_call(
        body,
        grid=(NUM_X,),
        in_specs=[
            pl.BlockSpec(memory_space=pltpu.SMEM),
            pl.BlockSpec((NUM_CORE * own, depth), lambda i: (i, 0)),
            pl.BlockSpec((groups, steps, part, cols), lambda i: (0, 0, 0, 0)),
        ],
        out_specs=[
            pl.BlockSpec((1, own, rhs), lambda i: (i, 0, 0)),
            pl.BlockSpec((1, own, rhs), lambda i: (i, 0, 0)),
        ],
        out_shape=[
            jax.ShapeDtypeStruct((NUM_X, own, rhs), F32),
            jax.ShapeDtypeStruct((NUM_X, own, rhs), BF16),
        ],
        scratch_shapes=[pltpu.VMEM((rhs, depth), BF16)],
        name="product",
    )(lax.axis_index("core").astype(jnp.int32)[None], factor, every)


def per_device(right_side, partial_in, window_factor, inverse_t, trailing_factor):
    steps, rows, rhs = right_side.shape
    cols = inverse_t.shape[2]
    part = rhs // NUM_Y
    slab = rows * NUM_Y
    trail_rows = trailing_factor.shape[0]

    first = (lax.axis_index(NARROW) == 0).astype(F32)
    terms = partial_in[0] - right_side.astype(F32) * first
    terms = terms.astype(BF16).reshape(steps, rows, NUM_Y, part).transpose(2, 0, 1, 3)
    terms = terms.reshape(NUM_Y, steps * rows * part // cols, cols)

    pairs = [(block, prior) for block in range(steps) for prior in range(block)]
    pieces = [window_factor[block, :, prior, :] for block, prior in pairs]
    pieces += [inverse_t[block] for block in range(steps)]
    pieces = jnp.concatenate(pieces)
    split = pieces.shape[0]
    copies = jnp.broadcast_to(pieces[None], (NUM_Y,) + pieces.shape)
    packed = lax.all_to_all(
        jnp.concatenate([copies, terms], axis=1), "y", 0, 0, tiled=True
    )
    terms = packed[:, split:].reshape(NUM_Y, steps, rows, part)
    terms = terms.transpose(1, 3, 0, 2).reshape(steps, part, slab).astype(F32)
    pieces = packed[:, :split].reshape(NUM_Y, -1, rows, cols)
    pieces = pieces.transpose(1, 0, 2, 3).reshape(-1, slab, cols)
    window = {pair: pieces[i] for i, pair in enumerate(pairs)}
    inverse = [pieces[len(pairs) + block] for block in range(steps)]

    solved_t = []
    for block in range(steps):
        fanned = terms[block]
        for prior in range(block):
            fanned = fanned + lax.dot_general(
                solved_t[prior], window[block, prior], (((1,), (1,)), ((), ())),
                preferred_element_type=F32,
            )
        fanned = total(spread(fanned.astype(BF16), NARROW, NUM_NARROW))
        residue = (-fanned).astype(BF16)
        share = jnp.dot(residue, inverse[block], preferred_element_type=F32)
        share = total(spread(share.astype(BF16), "z", NUM_Z))
        solved_t.append(share.astype(BF16))

    every = spread(jnp.stack(solved_t), "y", NUM_Y)
    solved = every.transpose(1, 3, 0, 2).reshape(steps, cols, rhs)

    flat_factor = trailing_factor.reshape(trail_rows, steps * cols)
    kept, away = product(flat_factor, every)
    back = lax.ppermute(away, "core", [(0, 1), (1, 0)])
    pair_sum = (kept + back.astype(F32)).astype(BF16)
    trailing = total(lax.all_to_all(pair_sum, "x", 0, 0, tiled=True))
    return (solved, trailing)


def solution(mesh):
    grid = Mesh(
        mesh.devices.reshape(NUM_Y, NUM_Z, NUM_X, NUM_CORE), ("y", "z", "x", "core")
    )
    wide = ("y", "z")
    placed = (
        P(None, wide, None),
        P(NARROW, None, wide, None),
        P(None, wide, None, NARROW),
        P(None, wide, NARROW),
        P(wide, None, NARROW),
    )
    return jax.shard_map(
        per_device,
        mesh=grid,
        in_specs=placed,
        out_specs=(P(None, NARROW, None), P(wide + NARROW, None)),
        check_vma=False,
    )
```

```python
import jax
import jax.numpy as jnp
from jax import lax
from jax.experimental import pallas as pl
from jax.experimental.pallas import tpu as pltpu
from jax.sharding import Mesh
from jax.sharding import PartitionSpec as P

F32 = jnp.float32
BF16 = jnp.bfloat16
NARROW = ("x", "core")
NUM_Y, NUM_Z, NUM_X, NUM_CORE = 8, 8, 4, 2
NUM_NARROW = NUM_X * NUM_CORE
SCRATCH = 8 * 2**20
ROWS_T = (((1,), (1,)), ((), ()))
VMEM = pl.BlockSpec(memory_space=pltpu.VMEM)
ANY = pl.BlockSpec(memory_space=pl.ANY)
SMEM = pl.BlockSpec(memory_space=pltpu.SMEM)


def resident(*arrays):
    return [pltpu.with_memory_space_constraint(array, pltpu.VMEM) for array in arrays]


def spread(value, axis, count):
    copies = jnp.broadcast_to(value[None], (count,) + value.shape)
    return lax.all_to_all(copies, axis, 0, 0, tiled=True)


def total(stack):
    return stack.astype(F32).sum(0)


def pairs_of(steps):
    return [(block, prior) for block in range(steps) for prior in range(block)]


def pack(right_side, partial_in, window_factor, inverse_t, first, ahead):
    steps, rows, rhs = right_side.shape
    cols = inverse_t.shape[2]
    part = rhs // NUM_Y
    pairs = pairs_of(steps)
    split = (len(pairs) + steps) * rows
    half = steps // 2

    def body(first_ref, right_ref, partial_ref, window_ref, inverse_ref, _, out_ref):
        for spot, (block, prior) in enumerate(pairs):
            piece = window_ref[block].astype(F32)[:, prior, :].astype(BF16)
            for y in range(NUM_Y):
                out_ref[y, spot * rows : (spot + 1) * rows, :] = piece
        for block in range(steps):
            spot = len(pairs) + block
            piece = inverse_ref[block]
            for y in range(NUM_Y):
                out_ref[y, spot * rows : (spot + 1) * rows, :] = piece
        taken = first_ref[0]
        for block in range(half):
            terms = [
                (partial_ref[0, k] - right_ref[k].astype(F32) * taken)
                for k in (block, block + half)
            ]
            spot = split + block * rows
            for y in range(NUM_Y):
                left, right = (t[:, y * part : (y + 1) * part] for t in terms)
                out_ref[y, spot : spot + rows, :] = jnp.concatenate(
                    [left, right], axis=1
                ).astype(BF16)

    return pl.pallas_call(
        body,
        in_specs=[SMEM, VMEM, VMEM, VMEM, VMEM, ANY],
        out_specs=VMEM,
        out_shape=pltpu.VMEM((NUM_Y, split + half * rows, cols), BF16),
        compiler_params=pltpu.CompilerParams(vmem_limit_bytes=SCRATCH),
        name="pack",
    )(first, right_side, partial_in, window_factor, inverse_t, ahead)


def unpack(packed, steps, rows, part):
    cols = packed.shape[2]
    slab = NUM_Y * rows
    pairs = pairs_of(steps)
    split = (len(pairs) + steps) * rows
    half = steps // 2

    def body(packed_ref, terms_ref, inverse_ref, *window_refs):
        for spot, (block, prior) in enumerate(pairs):
            for y in range(NUM_Y):
                window_refs[block - 1][
                    y * rows : (y + 1) * rows, prior * cols : (prior + 1) * cols
                ] = packed_ref[y, spot * rows : (spot + 1) * rows, :]
        for block in range(steps):
            spot = len(pairs) + block
            for y in range(NUM_Y):
                inverse_ref[block, y * rows : (y + 1) * rows, :] = packed_ref[
                    y, spot * rows : (spot + 1) * rows, :
                ]
        for block in range(half):
            spot = split + block * rows
            stack = jnp.concatenate(
                [packed_ref[y, spot : spot + rows, :] for y in range(NUM_Y)], axis=0
            )
            turned = stack.astype(F32).T
            terms_ref[block] = turned[:part]
            terms_ref[block + half] = turned[part:]

    outs = [
        pltpu.VMEM((steps, part, slab), F32),
        pltpu.VMEM((steps, slab, cols), BF16),
    ] + [pltpu.VMEM((slab, cols * k), BF16) for k in range(1, steps)]
    return pl.pallas_call(
        body,
        in_specs=[VMEM],
        out_specs=[VMEM] * len(outs),
        out_shape=outs,
        compiler_params=pltpu.CompilerParams(vmem_limit_bytes=SCRATCH),
        name="unpack",
    )(*resident(packed))


def turn(every):
    groups, steps, part, cols = every.shape

    def body(every_ref, out_ref):
        for step in range(steps):
            stack = jnp.concatenate(
                [every_ref[group, step] for group in range(groups)], axis=0
            )
            out_ref[step] = stack.T

    return pl.pallas_call(
        body,
        in_specs=[VMEM],
        out_specs=VMEM,
        out_shape=pltpu.HBM((steps, cols, groups * part), BF16),
        compiler_params=pltpu.CompilerParams(vmem_limit_bytes=SCRATCH),
        name="turn",
    )(*resident(every))


def product(core, factor, every, back=None):
    trail_rows, depth = factor.shape
    groups, steps, part, cols = every.shape
    rhs = groups * part
    own = trail_rows // NUM_NARROW

    def body(core_ref, factor_ref, every_ref, *refs):
        out_ref, flat_ref = refs[-2:]
        side = 1 - core_ref[0] if back is None else core_ref[0]
        for group in range(groups):
            for step in range(steps):
                flat_ref[
                    group * part : (group + 1) * part,
                    step * cols : (step + 1) * cols,
                ] = every_ref[group, step]

        @pl.loop(0, NUM_X)
        def _(i):
            row = pl.multiple_of((NUM_CORE * i + side) * own, own)
            value = lax.dot_general(
                factor_ref[pl.ds(row, own), :], flat_ref[...], ROWS_T,
                preferred_element_type=F32,
            )
            if back is not None:
                value = value + refs[0][i].astype(F32)
            out_ref[i] = value.astype(BF16)

    arrays = resident(factor, every) + ([] if back is None else resident(back[0]))
    after = []
    if back is not None:
        after = [pltpu.with_memory_space_constraint(back[1], pltpu.HBM)]
    return pl.pallas_call(
        body,
        in_specs=[SMEM] + [VMEM] * len(arrays) + [ANY] * len(after),
        out_specs=VMEM,
        scratch_shapes=[pltpu.VMEM((rhs, depth), BF16)],
        out_shape=pltpu.VMEM((NUM_X, own, rhs), BF16),
        compiler_params=pltpu.CompilerParams(vmem_limit_bytes=SCRATCH),
        name="product",
    )(core, *arrays, *after)


def per_device(right_side, partial_in, window_factor, inverse_t, trailing_factor):
    steps, rows, rhs = right_side.shape
    cols = inverse_t.shape[2]
    part = rhs // NUM_Y
    trail_rows = trailing_factor.shape[0]

    first = (lax.axis_index(NARROW) == 0).astype(F32)[None]
    flat_factor = trailing_factor.reshape(trail_rows, steps * cols)
    packed = pack(right_side, partial_in, window_factor, inverse_t, first, flat_factor)
    packed = lax.all_to_all(packed, "y", 0, 0, tiled=True)
    terms, inverse, *window = unpack(packed, steps, rows, part)

    solved_t = []
    for block in range(steps):
        fanned = terms[block]
        if block:
            fanned = fanned + lax.dot_general(
                jnp.concatenate(solved_t, axis=1), window[block - 1], ROWS_T,
                preferred_element_type=F32,
            )
        fanned = total(spread(fanned.astype(BF16), NARROW, NUM_NARROW))
        residue = (-fanned).astype(BF16)
        share = jnp.dot(residue, inverse[block], preferred_element_type=F32)
        share = total(spread(share.astype(BF16), "z", NUM_Z))
        solved_t.append(share.astype(BF16))

    every = spread(jnp.stack(solved_t), "y", NUM_Y)

    core = lax.axis_index("core").astype(jnp.int32)[None]
    away = product(core, flat_factor, every)
    back = lax.ppermute(away, "core", [(0, 1), (1, 0)])
    solved = turn(every)
    kept = product(core, flat_factor, every, (back, solved))
    trailing = total(lax.all_to_all(kept, "x", 0, 0, tiled=True))
    return (solved, trailing)


def solution(mesh):
    grid = Mesh(
        mesh.devices.reshape(NUM_Y, NUM_Z, NUM_X, NUM_CORE), ("y", "z", "x", "core")
    )
    wide = ("y", "z")
    placed = (
        P(None, wide, None),
        P(NARROW, None, wide, None),
        P(None, wide, None, NARROW),
        P(None, wide, NARROW),
        P(wide, None, NARROW),
    )
    return jax.shard_map(
        per_device,
        mesh=grid,
        in_specs=placed,
        out_specs=(P(None, NARROW, None), P(wide + NARROW, None)),
        check_vma=False,
    )
```

```python
import jax
import jax.numpy as jnp
from jax import lax
from jax.experimental import pallas as pl
from jax.experimental.pallas import tpu as pltpu
from jax.sharding import Mesh
from jax.sharding import PartitionSpec as P

F32 = jnp.float32
BF16 = jnp.bfloat16
NARROW = ("x", "core")
NUM_Y, NUM_Z, NUM_X, NUM_CORE = 8, 8, 4, 2
NUM_NARROW = NUM_X * NUM_CORE
STEPS = 4
SCRATCH = 8 * 2**20
ROWS_T = (((1,), (1,)), ((), ()))
VMEM = pl.BlockSpec(memory_space=pltpu.VMEM)
ANY = pl.BlockSpec(memory_space=pl.ANY)
SMEM = pl.BlockSpec(memory_space=pltpu.SMEM)


def resident(*arrays):
    return [pltpu.with_memory_space_constraint(array, pltpu.VMEM) for array in arrays]


def spread(value, axis, count):
    copies = jnp.broadcast_to(value[None], (count,) + value.shape)
    return lax.all_to_all(copies, axis, 0, 0, tiled=True)


def total(stack):
    return stack.astype(F32).sum(0)


def pairs_of(steps):
    return [(block, prior) for block in range(steps) for prior in range(block)]


def pack(right_side, partial_in, window_factor, inverse_t, first, ahead):
    steps, rows, rhs = right_side.shape
    cols = inverse_t.shape[2]
    part = rhs // NUM_Y
    pairs = pairs_of(steps)
    split = (len(pairs) + steps) * rows
    half = steps // 2

    def body(first_ref, right_ref, partial_ref, window_ref, inverse_ref, _, out_ref):
        for spot, (block, prior) in enumerate(pairs):
            piece = window_ref[block].astype(F32)[:, prior, :].astype(BF16)
            for y in range(NUM_Y):
                out_ref[y, spot * rows : (spot + 1) * rows, :] = piece
        for block in range(steps):
            spot = len(pairs) + block
            piece = inverse_ref[block]
            for y in range(NUM_Y):
                out_ref[y, spot * rows : (spot + 1) * rows, :] = piece
        taken = first_ref[0]
        for block in range(half):
            terms = [
                (partial_ref[0, k] - right_ref[k].astype(F32) * taken)
                for k in (block, block + half)
            ]
            spot = split + block * rows
            for y in range(NUM_Y):
                left, right = (t[:, y * part : (y + 1) * part] for t in terms)
                out_ref[y, spot : spot + rows, :] = jnp.concatenate(
                    [left, right], axis=1
                ).astype(BF16)

    return pl.pallas_call(
        body,
        in_specs=[SMEM, VMEM, VMEM, VMEM, VMEM, ANY],
        out_specs=VMEM,
        out_shape=pltpu.VMEM((NUM_Y, split + half * rows, cols), BF16),
        compiler_params=pltpu.CompilerParams(vmem_limit_bytes=SCRATCH),
        name="pack",
    )(first, right_side, partial_in, window_factor, inverse_t, ahead)


def unpack(packed, native, rows, part):
    cols = packed.shape[2]
    slab = NUM_Y * rows
    pairs = pairs_of(STEPS)
    split = (len(pairs) + STEPS) * rows

    def body(
        packed_ref, native_ref, early_ref, late_ref, inverse_ref,
        one_ref, two_ref, last_ref, own_ref,
    ):
        own_ref[...] = native_ref[2]
        target = {
            (1, 0): (one_ref, 0, 0),
            (2, 0): (two_ref, 0, 0),
            (2, 1): (two_ref, 0, cols),
            (3, 0): (two_ref, slab, 0),
            (3, 1): (two_ref, slab, cols),
            (3, 2): (last_ref, 0, 0),
        }
        for spot, pair in enumerate(pairs):
            ref, row, col = target[pair]
            for y in range(NUM_Y):
                ref[row + y * rows : row + (y + 1) * rows, col : col + cols] = (
                    packed_ref[y, spot * rows : (spot + 1) * rows, :]
                )
        for block in range(STEPS):
            spot = len(pairs) + block
            for y in range(NUM_Y):
                inverse_ref[block, y * rows : (y + 1) * rows, :] = packed_ref[
                    y, spot * rows : (spot + 1) * rows, :
                ]
        for block in range(2):
            spot = split + block * rows
            stack = jnp.concatenate(
                [packed_ref[y, spot : spot + rows, :] for y in range(NUM_Y)], axis=0
            )
            turned = stack.astype(F32).T
            early_ref[block] = turned[:part]
            late_ref[:, block * slab : (block + 1) * slab] = turned[part:]

    outs = [
        pltpu.VMEM((2, part, slab), F32),
        pltpu.VMEM((part, 2 * slab), F32),
        pltpu.VMEM((STEPS, slab, cols), BF16),
        pltpu.VMEM((slab, cols), BF16),
        pltpu.VMEM((2 * slab, 2 * cols), BF16),
        pltpu.VMEM((slab, cols), BF16),
        pltpu.VMEM((rows, cols), BF16),
    ]
    return pl.pallas_call(
        body,
        in_specs=[VMEM, VMEM],
        out_specs=[VMEM] * len(outs),
        out_shape=outs,
        compiler_params=pltpu.CompilerParams(vmem_limit_bytes=SCRATCH),
        name="unpack",
    )(*resident(packed, native))


def fan(terms, solved, window, ahead):
    part, cols = terms.shape[0], solved.shape[1]

    def body(terms_ref, solved_ref, window_ref, _, out_ref):
        value = terms_ref[...]
        for block in range(2):
            value = value + lax.dot_general(
                solved_ref[block * part : (block + 1) * part, :],
                window_ref[:, block * cols : (block + 1) * cols],
                ROWS_T, preferred_element_type=F32,
            )
        value = value.astype(BF16)
        for n in range(NUM_NARROW):
            out_ref[n] = value

    return pl.pallas_call(
        body,
        in_specs=[VMEM] * 3 + [ANY],
        out_specs=VMEM,
        out_shape=pltpu.VMEM((NUM_NARROW,) + terms.shape, BF16),
        compiler_params=pltpu.CompilerParams(vmem_limit_bytes=SCRATCH),
        name="fan",
    )(*resident(terms, solved, window), ahead)


def pair(fanned, inverse, early):
    part, wide_cols = fanned.shape[1:]
    slab, cols = inverse.shape[1:]
    rows = slab // NUM_Y

    def body(fanned_ref, inverse_ref, early_ref, out_ref):
        residue = fanned_ref[0].astype(F32)
        for n in range(1, NUM_NARROW):
            residue = residue + fanned_ref[n].astype(F32)
        residue = (-residue).astype(BF16)
        two, three = residue[:, :slab], residue[:, slab:]
        link = jnp.concatenate(
            [early_ref[y, 2 * part : 2 * part + rows, :] for y in range(NUM_Y)], axis=0
        )
        left = jnp.dot(two, inverse_ref[2], preferred_element_type=F32)
        right = jnp.dot(three, inverse_ref[3], preferred_element_type=F32)
        right = right + jnp.dot(two, link, preferred_element_type=F32)
        for z in range(NUM_Z):
            out_ref[z, :, :cols] = left.astype(BF16)
            out_ref[z, :, cols:] = right.astype(BF16)

    return pl.pallas_call(
        body,
        in_specs=[VMEM] * 3,
        out_specs=VMEM,
        out_shape=pltpu.VMEM((NUM_Z, part, 2 * cols), BF16),
        compiler_params=pltpu.CompilerParams(vmem_limit_bytes=SCRATCH),
        name="pair",
    )(*resident(fanned, inverse, early))


def flatten(early_ref, late_ref, flat_ref):
    part, late_cols = late_ref.shape[1:]
    cols = late_cols // 2
    for y in range(NUM_Y):
        span = slice(y * part, (y + 1) * part)
        for block in range(2):
            flat_ref[span, block * cols : (block + 1) * cols] = early_ref[
                y, block * part : (block + 1) * part, :
            ]
        flat_ref[span, 2 * cols :] = late_ref[y]


def turn(early, late):
    part, late_cols = late.shape[1:]
    rhs = NUM_Y * part
    cols = late_cols // 2

    def body(early_ref, late_ref, out_ref, flat_ref):
        flatten(early_ref, late_ref, flat_ref)
        for step in range(STEPS):
            out_ref[step] = flat_ref[:, step * cols : (step + 1) * cols].T

    return pl.pallas_call(
        body,
        in_specs=[VMEM, VMEM],
        out_specs=VMEM,
        scratch_shapes=[pltpu.VMEM((rhs, STEPS * cols), BF16)],
        out_shape=pltpu.HBM((STEPS, cols, rhs), BF16),
        compiler_params=pltpu.CompilerParams(vmem_limit_bytes=SCRATCH),
        name="turn",
    )(*resident(early, late))


def product(core, factor, early, late, back=None):
    trail_rows, depth = factor.shape
    rhs = NUM_Y * late.shape[1]
    own = trail_rows // NUM_NARROW

    def body(core_ref, factor_ref, early_ref, late_ref, *refs):
        out_ref, flat_ref = refs[-2:]
        side = 1 - core_ref[0] if back is None else core_ref[0]
        flatten(early_ref, late_ref, flat_ref)

        @pl.loop(0, NUM_X)
        def _(i):
            row = pl.multiple_of((NUM_CORE * i + side) * own, own)
            value = lax.dot_general(
                factor_ref[pl.ds(row, own), :], flat_ref[...], ROWS_T,
                preferred_element_type=F32,
            )
            if back is not None:
                value = value + refs[0][i].astype(F32)
            out_ref[i] = value.astype(BF16)

    arrays = resident(factor, early, late) + ([] if back is None else resident(back[0]))
    after = []
    if back is not None:
        after = [pltpu.with_memory_space_constraint(back[1], pltpu.HBM)]
    return pl.pallas_call(
        body,
        in_specs=[SMEM] + [VMEM] * len(arrays) + [ANY] * len(after),
        out_specs=VMEM,
        scratch_shapes=[pltpu.VMEM((rhs, depth), BF16)],
        out_shape=pltpu.VMEM((NUM_X, own, rhs), BF16),
        compiler_params=pltpu.CompilerParams(vmem_limit_bytes=SCRATCH),
        name="product",
    )(core, *arrays, *after)


def per_device(right_side, partial_in, window_factor, inverse_t, trailing_factor):
    steps, rows, rhs = right_side.shape
    cols = inverse_t.shape[2]
    part = rhs // NUM_Y
    trail_rows = trailing_factor.shape[0]

    first = (lax.axis_index(NARROW) == 0).astype(F32)[None]
    flat_factor = trailing_factor.reshape(trail_rows, steps * cols)
    packed = pack(right_side, partial_in, window_factor, inverse_t, first, flat_factor)
    packed = lax.all_to_all(packed, "y", 0, 0, tiled=True)
    first_terms, late_terms, inverse, window_one, window_two, window_last, own = unpack(
        packed, inverse_t, rows, part
    )

    def over_narrow(value):
        return total(spread(value.astype(BF16), NARROW, NUM_NARROW))

    residue = (-over_narrow(first_terms[0])).astype(BF16)
    share = jnp.dot(residue, inverse[0], preferred_element_type=F32).astype(BF16)
    got = spread(jnp.concatenate([share, own]), "z", NUM_Z)
    solved_0 = total(got[:, :part]).astype(BF16)
    ahead = got[:, part:].reshape(NUM_Z * rows, cols)

    fanned = first_terms[1] + lax.dot_general(
        solved_0, window_one, ROWS_T, preferred_element_type=F32
    )
    link = lax.dot_general(window_last, ahead, ROWS_T, preferred_element_type=F32)
    both = over_narrow(jnp.concatenate([fanned, link]))
    residue, link = (-both[:part]).astype(BF16), (-both[part:]).astype(BF16)
    share = jnp.dot(residue, inverse[1], preferred_element_type=F32).astype(BF16)
    link = lax.dot_general(
        link, inverse[3], (((0,), (0,)), ((), ())), preferred_element_type=F32
    )
    copies = jnp.broadcast_to(share[None], (NUM_Z,) + share.shape)
    link = link.astype(BF16).reshape(NUM_Z, rows, cols)
    got = lax.all_to_all(
        jnp.concatenate([copies, link], axis=1), "z", 0, 0, tiled=True
    )
    got = total(got).astype(BF16)

    stack = jnp.concatenate([solved_0, got])
    early = spread(stack, "y", NUM_Y)
    fanned = fan(late_terms, stack, window_two, early)
    fanned = lax.all_to_all(fanned, NARROW, 0, 0, tiled=True)
    share = pair(fanned, inverse, early)
    late = total(lax.all_to_all(share, "z", 0, 0, tiled=True)).astype(BF16)
    late = spread(late, "y", NUM_Y)

    core = lax.axis_index("core").astype(jnp.int32)[None]
    away = product(core, flat_factor, early, late)
    back = lax.ppermute(away, "core", [(0, 1), (1, 0)])
    solved = turn(early, late)
    kept = product(core, flat_factor, early, late, (back, solved))
    trailing = total(lax.all_to_all(kept, "x", 0, 0, tiled=True))
    return (solved, trailing)


def solution(mesh):
    grid = Mesh(
        mesh.devices.reshape(NUM_Y, NUM_Z, NUM_X, NUM_CORE), ("y", "z", "x", "core")
    )
    wide = ("y", "z")
    placed = (
        P(None, wide, None),
        P(NARROW, None, wide, None),
        P(None, wide, None, NARROW),
        P(None, wide, NARROW),
        P(wide, None, NARROW),
    )
    return jax.shard_map(
        per_device,
        mesh=grid,
        in_specs=placed,
        out_specs=(P(None, NARROW, None), P(wide + NARROW, None)),
        check_vma=False,
    )
```

```python
import jax
import jax.numpy as jnp
from jax import lax
from jax.experimental import pallas as pl
from jax.experimental.pallas import tpu as pltpu
from jax.sharding import Mesh
from jax.sharding import PartitionSpec as P

F32 = jnp.float32
BF16 = jnp.bfloat16
NARROW = ("x", "core")
NUM_Y, NUM_Z, NUM_X, NUM_CORE = 8, 8, 4, 2
NUM_NARROW = NUM_X * NUM_CORE
STEPS = 4
SCRATCH = 8 * 2**20
ROWS_T = (((1,), (1,)), ((), ()))
VMEM = pl.BlockSpec(memory_space=pltpu.VMEM)
ANY = pl.BlockSpec(memory_space=pl.ANY)
HBM = pl.BlockSpec(memory_space=pltpu.HBM)
SMEM = pl.BlockSpec(memory_space=pltpu.SMEM)


def resident(*arrays):
    return [pltpu.with_memory_space_constraint(array, pltpu.VMEM) for array in arrays]


def spread(value, axis, count):
    copies = jnp.broadcast_to(value[None], (count,) + value.shape)
    return lax.all_to_all(copies, axis, 0, 0, tiled=True)


def total(stack):
    return stack.astype(F32).sum(0)


def pairs_of(steps):
    return [(block, prior) for block in range(steps) for prior in range(block)]


def pack(right_side, partial_in, window_factor, inverse_t, first):
    steps, rows, rhs = right_side.shape
    cols = inverse_t.shape[2]
    part = rhs // NUM_Y
    pairs = pairs_of(steps)
    split = (len(pairs) + steps) * rows
    half = steps // 2

    def body(first_ref, *refs):
        sources, (out_ref, own_ref), held, sems = refs[:4], refs[4:6], refs[6:10], refs[10]
        loads = [
            pltpu.make_async_copy(source, target, sems.at[i])
            for i, (source, target) in enumerate(zip(sources, held))
        ]
        for load in loads:
            load.start()
        for load in loads:
            load.wait()
        right_ref, partial_ref, window_ref, inverse_ref = held
        own_ref[...] = inverse_ref[2]
        for spot, (block, prior) in enumerate(pairs):
            piece = window_ref[block].astype(F32)[:, prior, :].astype(BF16)
            for y in range(NUM_Y):
                out_ref[y, spot * rows : (spot + 1) * rows, :] = piece
        for block in range(steps):
            spot = len(pairs) + block
            piece = inverse_ref[block]
            for y in range(NUM_Y):
                out_ref[y, spot * rows : (spot + 1) * rows, :] = piece
        taken = first_ref[0]
        for block in range(half):
            terms = [
                (partial_ref[0, k] - right_ref[k].astype(F32) * taken)
                for k in (block, block + half)
            ]
            spot = split + block * rows
            for y in range(NUM_Y):
                left, right = (t[:, y * part : (y + 1) * part] for t in terms)
                out_ref[y, spot : spot + rows, :] = jnp.concatenate(
                    [left, right], axis=1
                ).astype(BF16)

    return pl.pallas_call(
        body,
        in_specs=[SMEM] + [HBM] * 4,
        out_specs=[VMEM] * 2,
        out_shape=[
            pltpu.VMEM((NUM_Y, split + half * rows, cols), BF16),
            pltpu.VMEM((rows, cols), BF16),
        ],
        scratch_shapes=[
            pltpu.VMEM(array.shape, array.dtype)
            for array in (right_side, partial_in, window_factor, inverse_t)
        ]
        + [pltpu.SemaphoreType.DMA((4,))],
        compiler_params=pltpu.CompilerParams(vmem_limit_bytes=SCRATCH),
        name="pack",
    )(
        first,
        *(
            pltpu.with_memory_space_constraint(array, pltpu.HBM)
            for array in (right_side, partial_in, window_factor, inverse_t)
        ),
    )


def unpack(packed, rows, part):
    cols = packed.shape[2]
    slab = NUM_Y * rows
    pairs = pairs_of(STEPS)
    split = (len(pairs) + STEPS) * rows

    def body(packed_ref, early_ref, late_ref, inverse_ref, one_ref, two_ref, last_ref):
        target = {
            (1, 0): (one_ref, 0, 0),
            (2, 0): (two_ref, 0, 0),
            (2, 1): (two_ref, 0, cols),
            (3, 0): (two_ref, slab, 0),
            (3, 1): (two_ref, slab, cols),
            (3, 2): (last_ref, 0, 0),
        }
        for spot, pair in enumerate(pairs):
            ref, row, col = target[pair]
            for y in range(NUM_Y):
                ref[row + y * rows : row + (y + 1) * rows, col : col + cols] = (
                    packed_ref[y, spot * rows : (spot + 1) * rows, :]
                )
        for block in range(STEPS):
            spot = len(pairs) + block
            for y in range(NUM_Y):
                inverse_ref[block, y * rows : (y + 1) * rows, :] = packed_ref[
                    y, spot * rows : (spot + 1) * rows, :
                ]
        for block in range(2):
            spot = split + block * rows
            stack = jnp.concatenate(
                [packed_ref[y, spot : spot + rows, :] for y in range(NUM_Y)], axis=0
            )
            turned = stack.astype(F32).T
            early_ref[block] = turned[:part]
            late_ref[:, block * slab : (block + 1) * slab] = turned[part:]

    outs = [
        pltpu.VMEM((2, part, slab), F32),
        pltpu.VMEM((part, 2 * slab), F32),
        pltpu.VMEM((STEPS, slab, cols), BF16),
        pltpu.VMEM((slab, cols), BF16),
        pltpu.VMEM((2 * slab, 2 * cols), BF16),
        pltpu.VMEM((slab, cols), BF16),
    ]
    return pl.pallas_call(
        body,
        in_specs=[VMEM],
        out_specs=[VMEM] * len(outs),
        out_shape=outs,
        compiler_params=pltpu.CompilerParams(vmem_limit_bytes=SCRATCH),
        name="unpack",
    )(*resident(packed))


def fan(terms, solved, window):
    part, cols = terms.shape[0], solved.shape[1]

    def body(terms_ref, solved_ref, window_ref, out_ref):
        value = terms_ref[...]
        for block in range(2):
            value = value + lax.dot_general(
                solved_ref[block * part : (block + 1) * part, :],
                window_ref[:, block * cols : (block + 1) * cols],
                ROWS_T, preferred_element_type=F32,
            )
        out_ref[...] = value.astype(BF16)

    return pl.pallas_call(
        body,
        in_specs=[VMEM] * 3,
        out_specs=VMEM,
        out_shape=pltpu.VMEM(terms.shape, BF16),
        compiler_params=pltpu.CompilerParams(vmem_limit_bytes=SCRATCH),
        name="fan",
    )(*resident(terms, solved, window))


def pair(fanned, inverse, early):
    part, wide_cols = fanned.shape[1:]
    slab, cols = inverse.shape[1:]
    rows = slab // NUM_Y

    def body(fanned_ref, inverse_ref, early_ref, out_ref):
        residue = fanned_ref[0].astype(F32)
        for n in range(1, NUM_NARROW):
            residue = residue + fanned_ref[n].astype(F32)
        residue = (-residue).astype(BF16)
        two, three = residue[:, :slab], residue[:, slab:]
        link = jnp.concatenate(
            [early_ref[y, 2 * part : 2 * part + rows, :] for y in range(NUM_Y)], axis=0
        )
        left = jnp.dot(two, inverse_ref[2], preferred_element_type=F32)
        right = jnp.dot(three, inverse_ref[3], preferred_element_type=F32)
        right = right + jnp.dot(two, link, preferred_element_type=F32)
        for z in range(NUM_Z):
            out_ref[z, :, :cols] = left.astype(BF16)
            out_ref[z, :, cols:] = right.astype(BF16)

    return pl.pallas_call(
        body,
        in_specs=[VMEM] * 3,
        out_specs=VMEM,
        out_shape=pltpu.VMEM((NUM_Z, part, 2 * cols), BF16),
        compiler_params=pltpu.CompilerParams(vmem_limit_bytes=SCRATCH),
        name="pair",
    )(*resident(fanned, inverse, early))


def flatten(early_ref, late_ref, flat_ref):
    part, late_cols = late_ref.shape[1:]
    cols = late_cols // 2
    for y in range(NUM_Y):
        span = slice(y * part, (y + 1) * part)
        for block in range(2):
            flat_ref[span, block * cols : (block + 1) * cols] = early_ref[
                y, block * part : (block + 1) * part, :
            ]
        flat_ref[span, 2 * cols :] = late_ref[y]


def turn(early, late):
    part, late_cols = late.shape[1:]
    rhs = NUM_Y * part
    cols = late_cols // 2

    def body(early_ref, late_ref, out_ref, flat_ref):
        flatten(early_ref, late_ref, flat_ref)
        for step in range(STEPS):
            out_ref[step] = flat_ref[:, step * cols : (step + 1) * cols].T

    return pl.pallas_call(
        body,
        in_specs=[VMEM, VMEM],
        out_specs=VMEM,
        scratch_shapes=[pltpu.VMEM((rhs, STEPS * cols), BF16)],
        out_shape=pltpu.HBM((STEPS, cols, rhs), BF16),
        compiler_params=pltpu.CompilerParams(vmem_limit_bytes=SCRATCH),
        name="turn",
    )(*resident(early, late))


def product(core, factor, early, late, back=None):
    trail_rows, steps, cols = factor.shape
    depth = steps * cols
    rhs = NUM_Y * late.shape[1]
    own = trail_rows // NUM_NARROW

    def body(core_ref, factor_ref, early_ref, late_ref, *refs):
        out_ref, flat_ref = refs[-2:]
        side = 1 - core_ref[0] if back is None else core_ref[0]
        flatten(early_ref, late_ref, flat_ref)

        def rows_of(start, i):
            value = lax.dot_general(
                factor_ref[start : start + own].reshape(own, depth), flat_ref[...],
                ROWS_T, preferred_element_type=F32,
            )
            if back is not None:
                value = value + refs[0][i].astype(F32)
            out_ref[i] = value.astype(BF16)

        for half in range(NUM_CORE):

            @pl.when(side == half)
            def _():
                for i in range(NUM_X):
                    rows_of((NUM_CORE * i + half) * own, i)

    arrays = resident(factor, early, late) + ([] if back is None else resident(back[0]))
    after = []
    if back is not None:
        after = [pltpu.with_memory_space_constraint(back[1], pltpu.HBM)]
    return pl.pallas_call(
        body,
        in_specs=[SMEM] + [VMEM] * len(arrays) + [ANY] * len(after),
        out_specs=VMEM,
        scratch_shapes=[pltpu.VMEM((rhs, depth), BF16)],
        out_shape=pltpu.VMEM((NUM_X, own, rhs), BF16),
        compiler_params=pltpu.CompilerParams(vmem_limit_bytes=SCRATCH),
        name="product",
    )(core, *arrays, *after)


def per_device(right_side, partial_in, window_factor, inverse_t, trailing_factor):
    steps, rows, rhs = right_side.shape
    cols = inverse_t.shape[2]
    part = rhs // NUM_Y
    trail_rows = trailing_factor.shape[0]

    first = (lax.axis_index(NARROW) == 0).astype(F32)[None]
    packed, own = pack(right_side, partial_in, window_factor, inverse_t, first)
    packed = lax.all_to_all(packed, "y", 0, 0, tiled=True)
    first_terms, late_terms, inverse, window_one, window_two, window_last = unpack(
        packed, rows, part
    )

    def over_narrow(value):
        return total(spread(value.astype(BF16), NARROW, NUM_NARROW))

    residue = (-over_narrow(first_terms[0])).astype(BF16)
    share = jnp.dot(residue, inverse[0], preferred_element_type=F32).astype(BF16)
    got = spread(jnp.concatenate([share, own]), "z", NUM_Z)
    solved_0 = total(got[:, :part]).astype(BF16)
    ahead = got[:, part:].reshape(NUM_Z * rows, cols)

    fanned = first_terms[1] + lax.dot_general(
        solved_0, window_one, ROWS_T, preferred_element_type=F32
    )
    link = lax.dot_general(window_last, ahead, ROWS_T, preferred_element_type=F32)
    both = over_narrow(jnp.concatenate([fanned, link]))
    residue, link = (-both[:part]).astype(BF16), (-both[part:]).astype(BF16)
    share = jnp.dot(residue, inverse[1], preferred_element_type=F32).astype(BF16)
    link = lax.dot_general(
        link, inverse[3], (((0,), (0,)), ((), ())), preferred_element_type=F32
    )
    copies = jnp.broadcast_to(share[None], (NUM_Z,) + share.shape)
    link = link.astype(BF16).reshape(NUM_Z, rows, cols)
    got = lax.all_to_all(
        jnp.concatenate([copies, link], axis=1), "z", 0, 0, tiled=True
    )
    got = total(got).astype(BF16)

    stack = jnp.concatenate([solved_0, got])
    early = spread(stack, "y", NUM_Y)
    fanned = lax.all_gather(fan(late_terms, stack, window_two), NARROW, axis=0)
    share = pair(fanned, inverse, early)
    late = total(lax.all_to_all(share, "z", 0, 0, tiled=True)).astype(BF16)
    late = spread(late, "y", NUM_Y)

    core = lax.axis_index("core").astype(jnp.int32)[None]
    away = product(core, trailing_factor, early, late)
    back = lax.ppermute(away, "core", [(0, 1), (1, 0)])
    solved = turn(early, late)
    kept = product(core, trailing_factor, early, late, (back, solved))
    trailing = total(lax.all_to_all(kept, "x", 0, 0, tiled=True))
    return (solved, trailing)


def solution(mesh):
    grid = Mesh(
        mesh.devices.reshape(NUM_Y, NUM_Z, NUM_X, NUM_CORE), ("y", "z", "x", "core")
    )
    wide = ("y", "z")
    placed = (
        P(None, wide, None),
        P(NARROW, None, wide, None),
        P(None, wide, None, NARROW),
        P(None, wide, NARROW),
        P(wide, None, NARROW),
    )
    return jax.shard_map(
        per_device,
        mesh=grid,
        in_specs=placed,
        out_specs=(P(None, NARROW, None), P(wide + NARROW, None)),
        check_vma=False,
    )
```

```python
import jax
import jax.numpy as jnp
from jax import lax
from jax.experimental import pallas as pl
from jax.experimental.pallas import tpu as pltpu
from jax.sharding import Mesh
from jax.sharding import PartitionSpec as P

F32 = jnp.float32
BF16 = jnp.bfloat16
NARROW = ("x", "core")
NUM_Y, NUM_Z, NUM_X, NUM_CORE = 8, 8, 4, 2
NUM_NARROW = NUM_X * NUM_CORE
STEPS = 4
SENT = (0, 1, 3)
SCRATCH = 8 * 2**20
ROWS_T = (((1,), (1,)), ((), ()))
VMEM = pl.BlockSpec(memory_space=pltpu.VMEM)
HBM = pl.BlockSpec(memory_space=pltpu.HBM)
SMEM = pl.BlockSpec(memory_space=pltpu.SMEM)


def resident(*arrays):
    return [pltpu.with_memory_space_constraint(array, pltpu.VMEM) for array in arrays]


def spread(value, axis, count):
    copies = jnp.broadcast_to(value[None], (count,) + value.shape)
    return lax.all_to_all(copies, axis, 0, 0, tiled=True)


def total(stack):
    return stack.astype(F32).sum(0)


def pairs_of(steps):
    return [(block, prior) for block in range(steps) for prior in range(block)]


def pack(right_side, partial_in, window_factor, inverse_t, first):
    steps, rows, rhs = right_side.shape
    cols = inverse_t.shape[2]
    part = rhs // NUM_Y
    pairs = pairs_of(steps)
    split = (len(pairs) + len(SENT)) * rows
    half = steps // 2

    def body(first_ref, *refs):
        sources, (out_ref, own_ref), held, sems = refs[:4], refs[4:6], refs[6:10], refs[10]
        loads = [
            pltpu.make_async_copy(source, target, sems.at[i])
            for i, (source, target) in enumerate(zip(sources, held))
        ]
        for load in loads:
            load.start()
        for load in loads:
            load.wait()
        right_ref, partial_ref, window_ref, inverse_ref = held
        own_ref[...] = inverse_ref[2]
        for spot, (block, prior) in enumerate(pairs):
            piece = window_ref[block].astype(F32)[:, prior, :].astype(BF16)
            for y in range(NUM_Y):
                out_ref[y, spot * rows : (spot + 1) * rows, :] = piece
        for spot, block in enumerate(SENT, len(pairs)):
            piece = inverse_ref[block]
            for y in range(NUM_Y):
                out_ref[y, spot * rows : (spot + 1) * rows, :] = piece
        taken = first_ref[0]
        for block in range(half):
            terms = [
                (partial_ref[0, k] - right_ref[k].astype(F32) * taken)
                for k in (block, block + half)
            ]
            spot = split + block * rows
            for y in range(NUM_Y):
                left, right = (t[:, y * part : (y + 1) * part] for t in terms)
                out_ref[y, spot : spot + rows, :] = jnp.concatenate(
                    [left, right], axis=1
                ).astype(BF16)

    return pl.pallas_call(
        body,
        in_specs=[SMEM] + [HBM] * 4,
        out_specs=[VMEM] * 2,
        out_shape=[
            pltpu.VMEM((NUM_Y, split + half * rows, cols), BF16),
            pltpu.VMEM((rows, cols), BF16),
        ],
        scratch_shapes=[
            pltpu.VMEM(array.shape, array.dtype)
            for array in (right_side, partial_in, window_factor, inverse_t)
        ]
        + [pltpu.SemaphoreType.DMA((4,))],
        compiler_params=pltpu.CompilerParams(vmem_limit_bytes=SCRATCH),
        name="pack",
    )(
        first,
        *(
            pltpu.with_memory_space_constraint(array, pltpu.HBM)
            for array in (right_side, partial_in, window_factor, inverse_t)
        ),
    )


def unpack(packed, rows, part):
    cols = packed.shape[2]
    slab = NUM_Y * rows
    pairs = pairs_of(STEPS)
    split = (len(pairs) + len(SENT)) * rows

    def body(packed_ref, early_ref, late_ref, inverse_ref, one_ref, two_ref, last_ref):
        target = {
            (1, 0): (one_ref, 0, 0),
            (2, 0): (two_ref, 0, 0),
            (2, 1): (two_ref, 0, cols),
            (3, 0): (two_ref, slab, 0),
            (3, 1): (two_ref, slab, cols),
            (3, 2): (last_ref, 0, 0),
        }
        for spot, pair in enumerate(pairs):
            ref, row, col = target[pair]
            for y in range(NUM_Y):
                ref[row + y * rows : row + (y + 1) * rows, col : col + cols] = (
                    packed_ref[y, spot * rows : (spot + 1) * rows, :]
                )
        for block in range(len(SENT)):
            spot = len(pairs) + block
            for y in range(NUM_Y):
                inverse_ref[block, y * rows : (y + 1) * rows, :] = packed_ref[
                    y, spot * rows : (spot + 1) * rows, :
                ]
        for block in range(2):
            spot = split + block * rows
            stack = jnp.concatenate(
                [packed_ref[y, spot : spot + rows, :] for y in range(NUM_Y)], axis=0
            )
            turned = stack.astype(F32).T
            early_ref[block] = turned[:part]
            late_ref[:, block * slab : (block + 1) * slab] = turned[part:]

    outs = [
        pltpu.VMEM((2, part, slab), F32),
        pltpu.VMEM((part, 2 * slab), F32),
        pltpu.VMEM((len(SENT), slab, cols), BF16),
        pltpu.VMEM((slab, cols), BF16),
        pltpu.VMEM((2 * slab, 2 * cols), BF16),
        pltpu.VMEM((slab, cols), BF16),
    ]
    return pl.pallas_call(
        body,
        in_specs=[VMEM],
        out_specs=[VMEM] * len(outs),
        out_shape=outs,
        compiler_params=pltpu.CompilerParams(vmem_limit_bytes=SCRATCH),
        name="unpack",
    )(*resident(packed))


def fan(terms, solved, window):
    part, cols = terms.shape[0], solved.shape[1]

    def body(terms_ref, solved_ref, window_ref, out_ref):
        value = terms_ref[...]
        for block in range(2):
            value = value + lax.dot_general(
                solved_ref[block * part : (block + 1) * part, :],
                window_ref[:, block * cols : (block + 1) * cols],
                ROWS_T, preferred_element_type=F32,
            )
        out_ref[...] = value.astype(BF16)

    return pl.pallas_call(
        body,
        in_specs=[VMEM] * 3,
        out_specs=VMEM,
        out_shape=pltpu.VMEM(terms.shape, BF16),
        compiler_params=pltpu.CompilerParams(vmem_limit_bytes=SCRATCH),
        name="fan",
    )(*resident(terms, solved, window))


def pair(fanned, inverse, early):
    part, wide_cols = fanned.shape[1:]
    slab, cols = inverse.shape[1:]
    rows = slab // NUM_Y

    def body(fanned_ref, inverse_ref, early_ref, out_ref):
        residue = fanned_ref[0].astype(F32)
        for n in range(1, NUM_NARROW):
            residue = residue + fanned_ref[n].astype(F32)
        residue = (-residue).astype(BF16)
        two, three = residue[:, :slab], residue[:, slab:]
        link, second = (
            jnp.concatenate(
                [early_ref[y, start : start + rows, :] for y in range(NUM_Y)], axis=0
            )
            for start in (2 * part, 2 * part + rows)
        )
        left = jnp.dot(two, second, preferred_element_type=F32)
        right = jnp.dot(three, inverse_ref[2], preferred_element_type=F32)
        right = right + jnp.dot(two, link, preferred_element_type=F32)
        for z in range(NUM_Z):
            out_ref[z, :, :cols] = left.astype(BF16)
            out_ref[z, :, cols:] = right.astype(BF16)

    return pl.pallas_call(
        body,
        in_specs=[VMEM] * 3,
        out_specs=VMEM,
        out_shape=pltpu.VMEM((NUM_Z, part, 2 * cols), BF16),
        compiler_params=pltpu.CompilerParams(vmem_limit_bytes=SCRATCH),
        name="pair",
    )(*resident(fanned, inverse, early))


def flatten(early_ref, late_ref, flat_ref):
    part, late_cols = late_ref.shape[1:]
    cols = late_cols // 2
    for y in range(NUM_Y):
        span = slice(y * part, (y + 1) * part)
        for block in range(2):
            flat_ref[span, block * cols : (block + 1) * cols] = early_ref[
                y, block * part : (block + 1) * part, :
            ]
        flat_ref[span, 2 * cols :] = late_ref[y]


def turn(early, late):
    part, late_cols = late.shape[1:]
    rhs = NUM_Y * part
    cols = late_cols // 2

    def body(early_ref, late_ref, out_ref, flat_ref):
        flatten(early_ref, late_ref, flat_ref)
        for step in range(STEPS):
            out_ref[step] = flat_ref[:, step * cols : (step + 1) * cols].T

    return pl.pallas_call(
        body,
        in_specs=[VMEM, VMEM],
        out_specs=VMEM,
        scratch_shapes=[pltpu.VMEM((rhs, STEPS * cols), BF16)],
        out_shape=pltpu.HBM((STEPS, cols, rhs), BF16),
        compiler_params=pltpu.CompilerParams(vmem_limit_bytes=SCRATCH),
        name="turn",
    )(*resident(early, late))


def product(core, factor, early, late, dtype):
    trail_rows, steps, cols = factor.shape
    depth = steps * cols
    rhs = NUM_Y * late.shape[1]
    own = trail_rows // NUM_NARROW

    def body(core_ref, factor_ref, early_ref, late_ref, out_ref, flat_ref):
        side = 1 - core_ref[0] if dtype == BF16 else core_ref[0]
        flatten(early_ref, late_ref, flat_ref)
        for half in range(NUM_CORE):

            @pl.when(side == half)
            def _():
                for i in range(NUM_X):
                    start = (NUM_CORE * i + half) * own
                    out_ref[i] = lax.dot_general(
                        factor_ref[start : start + own].reshape(own, depth),
                        flat_ref[...], ROWS_T, preferred_element_type=F32,
                    ).astype(dtype)

    return pl.pallas_call(
        body,
        in_specs=[SMEM] + [VMEM] * 3,
        out_specs=VMEM,
        scratch_shapes=[pltpu.VMEM((rhs, depth), BF16)],
        out_shape=pltpu.VMEM((NUM_X, own, rhs), dtype),
        compiler_params=pltpu.CompilerParams(vmem_limit_bytes=SCRATCH),
        name="product",
    )(core, *resident(factor, early, late))


def merge(kept, back, ahead):
    def body(kept_ref, back_ref, _, out_ref):
        for i in range(NUM_X):
            out_ref[i] = (kept_ref[i] + back_ref[i].astype(F32)).astype(BF16)

    return pl.pallas_call(
        body,
        in_specs=[VMEM, VMEM, HBM],
        out_specs=VMEM,
        out_shape=pltpu.VMEM(kept.shape, BF16),
        compiler_params=pltpu.CompilerParams(vmem_limit_bytes=SCRATCH),
        name="merge",
    )(*resident(kept, back), pltpu.with_memory_space_constraint(ahead, pltpu.HBM))


def per_device(right_side, partial_in, window_factor, inverse_t, trailing_factor):
    steps, rows, rhs = right_side.shape
    cols = inverse_t.shape[2]
    part = rhs // NUM_Y
    trail_rows = trailing_factor.shape[0]

    first = (lax.axis_index(NARROW) == 0).astype(F32)[None]
    packed, own = pack(right_side, partial_in, window_factor, inverse_t, first)
    packed = lax.all_to_all(packed, "y", 0, 0, tiled=True)
    first_terms, late_terms, inverse, window_one, window_two, window_last = unpack(
        packed, rows, part
    )

    def over_narrow(value):
        return total(spread(value.astype(BF16), NARROW, NUM_NARROW))

    residue = (-over_narrow(first_terms[0])).astype(BF16)
    share = jnp.dot(residue, inverse[0], preferred_element_type=F32).astype(BF16)
    got = spread(jnp.concatenate([share, own]), "z", NUM_Z)
    solved_0 = total(got[:, :part]).astype(BF16)
    ahead = got[:, part:].reshape(NUM_Z * rows, cols)

    fanned = first_terms[1] + lax.dot_general(
        solved_0, window_one, ROWS_T, preferred_element_type=F32
    )
    link = lax.dot_general(window_last, ahead, ROWS_T, preferred_element_type=F32)
    both = over_narrow(jnp.concatenate([fanned, link]))
    residue, link = (-both[:part]).astype(BF16), (-both[part:]).astype(BF16)
    share = jnp.dot(residue, inverse[1], preferred_element_type=F32).astype(BF16)
    link = lax.dot_general(
        link, inverse[2], (((0,), (0,)), ((), ())), preferred_element_type=F32
    )
    copies = jnp.broadcast_to(share[None], (NUM_Z,) + share.shape)
    link = link.astype(BF16).reshape(NUM_Z, rows, cols)
    got = lax.all_to_all(
        jnp.concatenate([copies, link], axis=1), "z", 0, 0, tiled=True
    )
    got = total(got).astype(BF16)

    stack = jnp.concatenate([solved_0, got, own])
    early = spread(stack, "y", NUM_Y)
    fanned = lax.all_gather(fan(late_terms, stack, window_two), NARROW, axis=0)
    share = pair(fanned, inverse, early)
    late = total(lax.all_to_all(share, "z", 0, 0, tiled=True)).astype(BF16)
    late = spread(late, "y", NUM_Y)

    core = lax.axis_index("core").astype(jnp.int32)[None]
    away = product(core, trailing_factor, early, late, BF16)
    back = lax.ppermute(away, "core", [(0, 1), (1, 0)])
    kept = product(core, trailing_factor, early, late, F32)
    solved = turn(early, late)
    kept = merge(kept, back, solved)
    trailing = total(lax.all_to_all(kept, "x", 0, 0, tiled=True))
    return (solved, trailing)


def solution(mesh):
    grid = Mesh(
        mesh.devices.reshape(NUM_Y, NUM_Z, NUM_X, NUM_CORE), ("y", "z", "x", "core")
    )
    wide = ("y", "z")
    placed = (
        P(None, wide, None),
        P(NARROW, None, wide, None),
        P(None, wide, None, NARROW),
        P(None, wide, NARROW),
        P(wide, None, NARROW),
    )
    return jax.shard_map(
        per_device,
        mesh=grid,
        in_specs=placed,
        out_specs=(P(None, NARROW, None), P(wide + NARROW, None)),
        check_vma=False,
    )
```

```python
import jax
import jax.numpy as jnp
from jax import lax
from jax.experimental import pallas as pl
from jax.experimental.pallas import tpu as pltpu
from jax.sharding import Mesh
from jax.sharding import PartitionSpec as P

F32 = jnp.float32
BF16 = jnp.bfloat16
NARROW = ("x", "core")
NUM_Y, NUM_Z, NUM_X, NUM_CORE = 8, 8, 4, 2
NUM_NARROW = NUM_X * NUM_CORE
STEPS = 4
SENT = (0, 1, 3)
SCRATCH = 8 * 2**20
ROWS_T = (((1,), (1,)), ((), ()))
VMEM = pl.BlockSpec(memory_space=pltpu.VMEM)
HBM = pl.BlockSpec(memory_space=pltpu.HBM)
SMEM = pl.BlockSpec(memory_space=pltpu.SMEM)


def resident(*arrays):
    return [pltpu.with_memory_space_constraint(array, pltpu.VMEM) for array in arrays]


def spread(value, axis, count):
    copies = jnp.broadcast_to(value[None], (count,) + value.shape)
    return lax.all_to_all(copies, axis, 0, 0, tiled=True)


def total(stack):
    return stack.astype(F32).sum(0)


def pairs_of(steps):
    return [(block, prior) for block in range(steps) for prior in range(block)]


def pack(right_side, partial_in, window_factor, inverse_t, first):
    steps, rows, rhs = right_side.shape
    cols = inverse_t.shape[2]
    part = rhs // NUM_Y
    pairs = pairs_of(steps)
    split = (len(pairs) + len(SENT)) * rows
    half = steps // 2

    def body(first_ref, *refs):
        sources, (out_ref, own_ref), held, sems = refs[:4], refs[4:6], refs[6:10], refs[10]
        loads = [
            pltpu.make_async_copy(source, target, sems.at[i])
            for i, (source, target) in enumerate(zip(sources, held))
        ]
        for load in loads:
            load.start()
        for load in loads:
            load.wait()
        right_ref, partial_ref, window_ref, inverse_ref = held
        own_ref[...] = inverse_ref[2]
        for spot, (block, prior) in enumerate(pairs):
            piece = window_ref[block].astype(F32)[:, prior, :].astype(BF16)
            for y in range(NUM_Y):
                out_ref[y, spot * rows : (spot + 1) * rows, :] = piece
        for spot, block in enumerate(SENT, len(pairs)):
            piece = inverse_ref[block]
            for y in range(NUM_Y):
                out_ref[y, spot * rows : (spot + 1) * rows, :] = piece
        taken = first_ref[0]
        for block in range(half):
            terms = [
                (partial_ref[0, k] - right_ref[k].astype(F32) * taken)
                for k in (block, block + half)
            ]
            spot = split + block * rows
            for y in range(NUM_Y):
                left, right = (t[:, y * part : (y + 1) * part] for t in terms)
                out_ref[y, spot : spot + rows, :] = jnp.concatenate(
                    [left, right], axis=1
                ).astype(BF16)

    return pl.pallas_call(
        body,
        in_specs=[SMEM] + [HBM] * 4,
        out_specs=[VMEM] * 2,
        out_shape=[
            pltpu.VMEM((NUM_Y, split + half * rows, cols), BF16),
            pltpu.VMEM((rows, cols), BF16),
        ],
        scratch_shapes=[
            pltpu.VMEM(array.shape, array.dtype)
            for array in (right_side, partial_in, window_factor, inverse_t)
        ]
        + [pltpu.SemaphoreType.DMA((4,))],
        compiler_params=pltpu.CompilerParams(vmem_limit_bytes=SCRATCH),
        name="pack",
    )(
        first,
        *(
            pltpu.with_memory_space_constraint(array, pltpu.HBM)
            for array in (right_side, partial_in, window_factor, inverse_t)
        ),
    )


def unpack(packed, rows, part):
    cols = packed.shape[2]
    slab = NUM_Y * rows
    pairs = pairs_of(STEPS)
    split = (len(pairs) + len(SENT)) * rows

    def body(packed_ref, early_ref, late_ref, inverse_ref, one_ref, two_ref, last_ref):
        target = {
            (1, 0): (one_ref, 0, 0),
            (2, 0): (two_ref, 0, 0),
            (2, 1): (two_ref, 0, cols),
            (3, 0): (two_ref, slab, 0),
            (3, 1): (two_ref, slab, cols),
            (3, 2): (last_ref, 0, 0),
        }
        for spot, pair in enumerate(pairs):
            ref, row, col = target[pair]
            for y in range(NUM_Y):
                ref[row + y * rows : row + (y + 1) * rows, col : col + cols] = (
                    packed_ref[y, spot * rows : (spot + 1) * rows, :]
                )
        for block in range(len(SENT)):
            spot = len(pairs) + block
            for y in range(NUM_Y):
                inverse_ref[block, y * rows : (y + 1) * rows, :] = packed_ref[
                    y, spot * rows : (spot + 1) * rows, :
                ]
        for block in range(2):
            spot = split + block * rows
            stack = jnp.concatenate(
                [packed_ref[y, spot : spot + rows, :] for y in range(NUM_Y)], axis=0
            )
            turned = stack.astype(F32).T
            early_ref[block] = turned[:part]
            late_ref[:, block * slab : (block + 1) * slab] = turned[part:]

    outs = [
        pltpu.VMEM((2, part, slab), F32),
        pltpu.VMEM((part, 2 * slab), F32),
        pltpu.VMEM((len(SENT), slab, cols), BF16),
        pltpu.VMEM((slab, cols), BF16),
        pltpu.VMEM((2 * slab, 2 * cols), BF16),
        pltpu.VMEM((slab, cols), BF16),
    ]
    return pl.pallas_call(
        body,
        in_specs=[VMEM],
        out_specs=[VMEM] * len(outs),
        out_shape=outs,
        compiler_params=pltpu.CompilerParams(vmem_limit_bytes=SCRATCH),
        name="unpack",
    )(*resident(packed))


def summed(ref, rows=slice(None)):
    value = ref[0, rows, :].astype(F32)
    for i in range(1, ref.shape[0]):
        value = value + ref[i, rows, :].astype(F32)
    return value


def stage(body, outs, *arrays):
    return pl.pallas_call(
        body,
        in_specs=[VMEM] * len(arrays),
        out_specs=[VMEM] * len(outs),
        out_shape=[pltpu.VMEM(shape, BF16) for shape in outs],
        compiler_params=pltpu.CompilerParams(vmem_limit_bytes=SCRATCH),
        name=body.__name__,
    )(*resident(*arrays))


def step_zero(fanned, inverse, own):
    part, cols = fanned.shape[1:]
    rows = own.shape[0]

    def zero(fanned_ref, inverse_ref, own_ref, out_ref):
        residue = (-summed(fanned_ref)).astype(BF16)
        share = jnp.dot(residue, inverse_ref[0], preferred_element_type=F32)
        share = share.astype(BF16)
        for z in range(NUM_Z):
            out_ref[z, :part, :] = share
            out_ref[z, part:, :] = own_ref[...]

    return stage(zero, [(NUM_Z, part + rows, cols)], fanned, inverse, own)[0]


def step_one_fan(got, terms, window_one, window_last):
    part, slab = terms.shape[1:]
    cols = got.shape[2]
    rows = got.shape[1] - part

    def one_fan(got_ref, terms_ref, one_ref, last_ref, solved_ref, out_ref):
        solved = summed(got_ref, slice(0, part)).astype(BF16)
        solved_ref[...] = solved
        ahead = jnp.concatenate(
            [got_ref[z, part : part + rows, :] for z in range(NUM_Z)], axis=0
        )
        fanned = terms_ref[1] + lax.dot_general(
            solved, one_ref[...], ROWS_T, preferred_element_type=F32
        )
        link = lax.dot_general(
            last_ref[...], ahead, ROWS_T, preferred_element_type=F32
        )
        for n in range(NUM_NARROW):
            out_ref[n, :part, :] = fanned.astype(BF16)
            out_ref[n, part:, :] = link.astype(BF16)

    outs = [(part, cols), (NUM_NARROW, part + slab, slab)]
    return stage(one_fan, outs, got, terms, window_one, window_last)


def step_one(both, inverse, part, rows):
    cols = inverse.shape[2]

    def one(both_ref, inverse_ref, out_ref):
        value = (-summed(both_ref)).astype(BF16)
        share = jnp.dot(value[:part], inverse_ref[1], preferred_element_type=F32)
        link = lax.dot_general(
            value[part:], inverse_ref[2], (((0,), (0,)), ((), ())),
            preferred_element_type=F32,
        )
        for z in range(NUM_Z):
            out_ref[z, :part, :] = share.astype(BF16)
            out_ref[z, part:, :] = link[z * rows : (z + 1) * rows].astype(BF16)

    return stage(one, [(NUM_Z, part + rows, cols)], both, inverse)[0]


def fan(terms, solved, window):
    part, cols = terms.shape[0], solved.shape[1]

    def body(terms_ref, solved_ref, window_ref, out_ref):
        value = terms_ref[...]
        for block in range(2):
            value = value + lax.dot_general(
                solved_ref[block * part : (block + 1) * part, :],
                window_ref[:, block * cols : (block + 1) * cols],
                ROWS_T, preferred_element_type=F32,
            )
        out_ref[...] = value.astype(BF16)

    return pl.pallas_call(
        body,
        in_specs=[VMEM] * 3,
        out_specs=VMEM,
        out_shape=pltpu.VMEM(terms.shape, BF16),
        compiler_params=pltpu.CompilerParams(vmem_limit_bytes=SCRATCH),
        name="fan",
    )(*resident(terms, solved, window))


def pair(fanned, inverse, early):
    part, wide_cols = fanned.shape[1:]
    slab, cols = inverse.shape[1:]
    rows = slab // NUM_Y

    def body(fanned_ref, inverse_ref, early_ref, out_ref):
        residue = fanned_ref[0].astype(F32)
        for n in range(1, NUM_NARROW):
            residue = residue + fanned_ref[n].astype(F32)
        residue = (-residue).astype(BF16)
        two, three = residue[:, :slab], residue[:, slab:]
        link, second = (
            jnp.concatenate(
                [early_ref[y, start : start + rows, :] for y in range(NUM_Y)], axis=0
            )
            for start in (2 * part, 2 * part + rows)
        )
        left = jnp.dot(two, second, preferred_element_type=F32)
        right = jnp.dot(three, inverse_ref[2], preferred_element_type=F32)
        right = right + jnp.dot(two, link, preferred_element_type=F32)
        for z in range(NUM_Z):
            out_ref[z, :, :cols] = left.astype(BF16)
            out_ref[z, :, cols:] = right.astype(BF16)

    return pl.pallas_call(
        body,
        in_specs=[VMEM] * 3,
        out_specs=VMEM,
        out_shape=pltpu.VMEM((NUM_Z, part, 2 * cols), BF16),
        compiler_params=pltpu.CompilerParams(vmem_limit_bytes=SCRATCH),
        name="pair",
    )(*resident(fanned, inverse, early))


def flatten(early_ref, late_ref, flat_ref):
    part, late_cols = late_ref.shape[1:]
    cols = late_cols // 2
    for y in range(NUM_Y):
        span = slice(y * part, (y + 1) * part)
        for block in range(2):
            flat_ref[span, block * cols : (block + 1) * cols] = early_ref[
                y, block * part : (block + 1) * part, :
            ]
        flat_ref[span, 2 * cols :] = late_ref[y]


def turn(early, late):
    part, late_cols = late.shape[1:]
    rhs = NUM_Y * part
    cols = late_cols // 2

    def body(early_ref, late_ref, out_ref, flat_ref):
        flatten(early_ref, late_ref, flat_ref)
        for step in range(STEPS):
            out_ref[step] = flat_ref[:, step * cols : (step + 1) * cols].T

    return pl.pallas_call(
        body,
        in_specs=[VMEM, VMEM],
        out_specs=VMEM,
        scratch_shapes=[pltpu.VMEM((rhs, STEPS * cols), BF16)],
        out_shape=pltpu.HBM((STEPS, cols, rhs), BF16),
        compiler_params=pltpu.CompilerParams(vmem_limit_bytes=SCRATCH),
        name="turn",
    )(*resident(early, late))


def product(core, factor, early, late, dtype):
    trail_rows, steps, cols = factor.shape
    depth = steps * cols
    rhs = NUM_Y * late.shape[1]
    own = trail_rows // NUM_NARROW

    def body(core_ref, factor_ref, early_ref, late_ref, out_ref, flat_ref):
        side = 1 - core_ref[0] if dtype == BF16 else core_ref[0]
        flatten(early_ref, late_ref, flat_ref)
        for half in range(NUM_CORE):

            @pl.when(side == half)
            def _():
                for i in range(NUM_X):
                    start = (NUM_CORE * i + half) * own
                    out_ref[i] = lax.dot_general(
                        factor_ref[start : start + own].reshape(own, depth),
                        flat_ref[...], ROWS_T, preferred_element_type=F32,
                    ).astype(dtype)

    return pl.pallas_call(
        body,
        in_specs=[SMEM] + [VMEM] * 3,
        out_specs=VMEM,
        scratch_shapes=[pltpu.VMEM((rhs, depth), BF16)],
        out_shape=pltpu.VMEM((NUM_X, own, rhs), dtype),
        compiler_params=pltpu.CompilerParams(vmem_limit_bytes=SCRATCH),
        name="product",
    )(core, *resident(factor, early, late))


def merge(kept, back, ahead):
    def body(kept_ref, back_ref, _, out_ref):
        for i in range(NUM_X):
            out_ref[i] = (kept_ref[i] + back_ref[i].astype(F32)).astype(BF16)

    return pl.pallas_call(
        body,
        in_specs=[VMEM, VMEM, HBM],
        out_specs=VMEM,
        out_shape=pltpu.VMEM(kept.shape, BF16),
        compiler_params=pltpu.CompilerParams(vmem_limit_bytes=SCRATCH),
        name="merge",
    )(*resident(kept, back), pltpu.with_memory_space_constraint(ahead, pltpu.HBM))


def per_device(right_side, partial_in, window_factor, inverse_t, trailing_factor):
    steps, rows, rhs = right_side.shape
    cols = inverse_t.shape[2]
    part = rhs // NUM_Y
    trail_rows = trailing_factor.shape[0]

    first = (lax.axis_index(NARROW) == 0).astype(F32)[None]
    packed, own = pack(right_side, partial_in, window_factor, inverse_t, first)
    packed = lax.all_to_all(packed, "y", 0, 0, tiled=True)
    first_terms, late_terms, inverse, window_one, window_two, window_last = unpack(
        packed, rows, part
    )

    fanned = spread(first_terms[0].astype(BF16), NARROW, NUM_NARROW)
    got = step_zero(fanned, inverse, own)
    got = lax.all_to_all(got, "z", 0, 0, tiled=True)

    solved_0, both = step_one_fan(got, first_terms, window_one, window_last)
    both = lax.all_to_all(both, NARROW, 0, 0, tiled=True)
    got = step_one(both, inverse, part, rows)
    got = total(lax.all_to_all(got, "z", 0, 0, tiled=True)).astype(BF16)

    stack = jnp.concatenate([solved_0, got, own])
    early = spread(stack, "y", NUM_Y)
    fanned = lax.all_gather(fan(late_terms, stack, window_two), NARROW, axis=0)
    share = pair(fanned, inverse, early)
    late = total(lax.all_to_all(share, "z", 0, 0, tiled=True)).astype(BF16)
    late = spread(late, "y", NUM_Y)

    core = lax.axis_index("core").astype(jnp.int32)[None]
    away = product(core, trailing_factor, early, late, BF16)
    back = lax.ppermute(away, "core", [(0, 1), (1, 0)])
    kept = product(core, trailing_factor, early, late, F32)
    solved = turn(early, late)
    kept = merge(kept, back, solved)
    trailing = total(lax.all_to_all(kept, "x", 0, 0, tiled=True))
    return (solved, trailing)


def solution(mesh):
    grid = Mesh(
        mesh.devices.reshape(NUM_Y, NUM_Z, NUM_X, NUM_CORE), ("y", "z", "x", "core")
    )
    wide = ("y", "z")
    placed = (
        P(None, wide, None),
        P(NARROW, None, wide, None),
        P(None, wide, None, NARROW),
        P(None, wide, NARROW),
        P(wide, None, NARROW),
    )
    return jax.shard_map(
        per_device,
        mesh=grid,
        in_specs=placed,
        out_specs=(P(None, NARROW, None), P(wide + NARROW, None)),
        check_vma=False,
    )
```

```python
import jax
import jax.numpy as jnp
from jax import lax
from jax.experimental import pallas as pl
from jax.experimental.pallas import tpu as pltpu
from jax.sharding import Mesh
from jax.sharding import PartitionSpec as P

F32 = jnp.float32
BF16 = jnp.bfloat16
NARROW = ("x", "core")
NUM_Y, NUM_Z, NUM_X, NUM_CORE = 8, 8, 4, 2
NUM_NARROW = NUM_X * NUM_CORE
STEPS = 4
SENT = (0, 1, 3)
SCRATCH = 8 * 2**20
ROWS_T = (((1,), (1,)), ((), ()))
VMEM = pl.BlockSpec(memory_space=pltpu.VMEM)
HBM = pl.BlockSpec(memory_space=pltpu.HBM)
SMEM = pl.BlockSpec(memory_space=pltpu.SMEM)


def resident(*arrays):
    return [pltpu.with_memory_space_constraint(array, pltpu.VMEM) for array in arrays]


def spread(value, axis, count):
    copies = jnp.broadcast_to(value[None], (count,) + value.shape)
    return lax.all_to_all(copies, axis, 0, 0, tiled=True)


def total(stack):
    return stack.astype(F32).sum(0)


def pairs_of(steps):
    return [(block, prior) for block in range(steps) for prior in range(block)]


def pack(right_side, partial_in, window_factor, inverse_t, first):
    steps, rows, rhs = right_side.shape
    cols = inverse_t.shape[2]
    part = rhs // NUM_Y
    pairs = pairs_of(steps)
    split = (len(pairs) + len(SENT)) * rows
    half = steps // 2

    def body(first_ref, *refs):
        sources, (out_ref, own_ref), held, sems = refs[:4], refs[4:6], refs[6:10], refs[10]
        loads = [
            pltpu.make_async_copy(source, target, sems.at[i])
            for i, (source, target) in enumerate(zip(sources, held))
        ]
        for load in loads:
            load.start()
        for load in loads:
            load.wait()
        right_ref, partial_ref, window_ref, inverse_ref = held
        own_ref[...] = inverse_ref[2]
        for spot, (block, prior) in enumerate(pairs):
            piece = window_ref[block].astype(F32)[:, prior, :].astype(BF16)
            for y in range(NUM_Y):
                out_ref[y, spot * rows : (spot + 1) * rows, :] = piece
        for spot, block in enumerate(SENT, len(pairs)):
            piece = inverse_ref[block]
            for y in range(NUM_Y):
                out_ref[y, spot * rows : (spot + 1) * rows, :] = piece
        taken = first_ref[0]
        for block in range(half):
            terms = [
                (partial_ref[0, k] - right_ref[k].astype(F32) * taken)
                for k in (block, block + half)
            ]
            spot = split + block * rows
            for y in range(NUM_Y):
                left, right = (t[:, y * part : (y + 1) * part] for t in terms)
                out_ref[y, spot : spot + rows, :] = jnp.concatenate(
                    [left, right], axis=1
                ).astype(BF16)

    return pl.pallas_call(
        body,
        in_specs=[SMEM] + [HBM] * 4,
        out_specs=[VMEM] * 2,
        out_shape=[
            pltpu.VMEM((NUM_Y, split + half * rows, cols), BF16),
            pltpu.VMEM((rows, cols), BF16),
        ],
        scratch_shapes=[
            pltpu.VMEM(array.shape, array.dtype)
            for array in (right_side, partial_in, window_factor, inverse_t)
        ]
        + [pltpu.SemaphoreType.DMA((4,))],
        compiler_params=pltpu.CompilerParams(vmem_limit_bytes=SCRATCH),
        name="pack",
    )(
        first,
        *(
            pltpu.with_memory_space_constraint(array, pltpu.HBM)
            for array in (right_side, partial_in, window_factor, inverse_t)
        ),
    )


def unpack(packed, rows, part):
    cols = packed.shape[2]
    slab = NUM_Y * rows
    pairs = pairs_of(STEPS)
    split = (len(pairs) + len(SENT)) * rows

    def body(packed_ref, early_ref, late_ref, inverse_ref, one_ref, two_ref, last_ref):
        target = {
            (1, 0): (one_ref, 0, 0),
            (2, 0): (two_ref, 0, 0),
            (2, 1): (two_ref, 0, cols),
            (3, 0): (two_ref, slab, 0),
            (3, 1): (two_ref, slab, cols),
            (3, 2): (last_ref, 0, 0),
        }
        for spot, pair in enumerate(pairs):
            ref, row, col = target[pair]
            for y in range(NUM_Y):
                ref[row + y * rows : row + (y + 1) * rows, col : col + cols] = (
                    packed_ref[y, spot * rows : (spot + 1) * rows, :]
                )
        for block in range(len(SENT)):
            spot = len(pairs) + block
            for y in range(NUM_Y):
                inverse_ref[block, y * rows : (y + 1) * rows, :] = packed_ref[
                    y, spot * rows : (spot + 1) * rows, :
                ]
        for block in range(2):
            spot = split + block * rows
            stack = jnp.concatenate(
                [packed_ref[y, spot : spot + rows, :] for y in range(NUM_Y)], axis=0
            )
            turned = stack.astype(F32).T
            early_ref[block] = turned[:part]
            late_ref[:, block * slab : (block + 1) * slab] = turned[part:]

    outs = [
        pltpu.VMEM((2, part, slab), F32),
        pltpu.VMEM((part, 2 * slab), F32),
        pltpu.VMEM((len(SENT), slab, cols), BF16),
        pltpu.VMEM((slab, cols), BF16),
        pltpu.VMEM((2 * slab, 2 * cols), BF16),
        pltpu.VMEM((slab, cols), BF16),
    ]
    return pl.pallas_call(
        body,
        in_specs=[VMEM],
        out_specs=[VMEM] * len(outs),
        out_shape=outs,
        compiler_params=pltpu.CompilerParams(vmem_limit_bytes=SCRATCH),
        name="unpack",
    )(*resident(packed))


def summed(ref, rows=slice(None)):
    value = ref[0, rows, :].astype(F32)
    for i in range(1, ref.shape[0]):
        value = value + ref[i, rows, :].astype(F32)
    return value


def stage(body, outs, *arrays):
    return pl.pallas_call(
        body,
        in_specs=[VMEM] * len(arrays),
        out_specs=[VMEM] * len(outs),
        out_shape=[pltpu.VMEM(shape, BF16) for shape in outs],
        compiler_params=pltpu.CompilerParams(vmem_limit_bytes=SCRATCH),
        name=body.__name__,
    )(*resident(*arrays))


def step_zero(fanned, inverse, own):
    part, cols = fanned.shape[1:]
    rows = own.shape[0]

    def zero(fanned_ref, inverse_ref, own_ref, out_ref):
        residue = (-summed(fanned_ref)).astype(BF16)
        share = jnp.dot(residue, inverse_ref[0], preferred_element_type=F32)
        share = share.astype(BF16)
        for z in range(NUM_Z):
            out_ref[z, :part, :] = share
            out_ref[z, part:, :] = own_ref[...]

    return stage(zero, [(NUM_Z, part + rows, cols)], fanned, inverse, own)[0]


def step_one_fan(got, terms, window_one, window_last):
    part, slab = terms.shape[1:]
    cols = got.shape[2]
    rows = got.shape[1] - part

    def one_fan(got_ref, terms_ref, one_ref, last_ref, solved_ref, out_ref):
        solved = summed(got_ref, slice(0, part)).astype(BF16)
        solved_ref[...] = solved
        ahead = jnp.concatenate(
            [got_ref[z, part : part + rows, :] for z in range(NUM_Z)], axis=0
        )
        fanned = terms_ref[1] + lax.dot_general(
            solved, one_ref[...], ROWS_T, preferred_element_type=F32
        )
        link = lax.dot_general(
            last_ref[...], ahead, ROWS_T, preferred_element_type=F32
        )
        for n in range(NUM_NARROW):
            out_ref[n, :part, :] = fanned.astype(BF16)
            out_ref[n, part:, :] = link.astype(BF16)

    outs = [(part, cols), (NUM_NARROW, part + slab, slab)]
    return stage(one_fan, outs, got, terms, window_one, window_last)


def step_one(both, inverse, part, rows):
    cols = inverse.shape[2]

    def one(both_ref, inverse_ref, out_ref):
        value = (-summed(both_ref)).astype(BF16)
        share = jnp.dot(value[:part], inverse_ref[1], preferred_element_type=F32)
        link = lax.dot_general(
            value[part:], inverse_ref[2], (((0,), (0,)), ((), ())),
            preferred_element_type=F32,
        )
        for z in range(NUM_Z):
            out_ref[z, :part, :] = share.astype(BF16)
            out_ref[z, part:, :] = link[z * rows : (z + 1) * rows].astype(BF16)

    return stage(one, [(NUM_Z, part + rows, cols)], both, inverse)[0]


def fan(terms, solved, window):
    part, cols = terms.shape[0], solved.shape[1]

    def body(terms_ref, solved_ref, window_ref, out_ref):
        value = terms_ref[...]
        for block in range(2):
            value = value + lax.dot_general(
                solved_ref[block * part : (block + 1) * part, :],
                window_ref[:, block * cols : (block + 1) * cols],
                ROWS_T, preferred_element_type=F32,
            )
        out_ref[...] = value.astype(BF16)

    return pl.pallas_call(
        body,
        in_specs=[VMEM] * 3,
        out_specs=VMEM,
        out_shape=pltpu.VMEM(terms.shape, BF16),
        compiler_params=pltpu.CompilerParams(vmem_limit_bytes=SCRATCH),
        name="fan",
    )(*resident(terms, solved, window))


def pair(fanned, inverse, early):
    part, wide_cols = fanned.shape[1:]
    slab, cols = inverse.shape[1:]
    rows = slab // NUM_Y

    def body(fanned_ref, inverse_ref, early_ref, out_ref):
        residue = fanned_ref[0].astype(F32)
        for n in range(1, NUM_NARROW):
            residue = residue + fanned_ref[n].astype(F32)
        residue = (-residue).astype(BF16)
        two, three = residue[:, :slab], residue[:, slab:]
        link, second = (
            jnp.concatenate(
                [early_ref[y, start : start + rows, :] for y in range(NUM_Y)], axis=0
            )
            for start in (2 * part, 2 * part + rows)
        )
        left = jnp.dot(two, second, preferred_element_type=F32)
        right = jnp.dot(three, inverse_ref[2], preferred_element_type=F32)
        right = right + jnp.dot(two, link, preferred_element_type=F32)
        for z in range(NUM_Z):
            out_ref[z, :, :cols] = left.astype(BF16)
            out_ref[z, :, cols:] = right.astype(BF16)

    return pl.pallas_call(
        body,
        in_specs=[VMEM] * 3,
        out_specs=VMEM,
        out_shape=pltpu.VMEM((NUM_Z, part, 2 * cols), BF16),
        compiler_params=pltpu.CompilerParams(vmem_limit_bytes=SCRATCH),
        name="pair",
    )(*resident(fanned, inverse, early))


def flatten(early_ref, late_ref, flat_ref):
    part, late_cols = late_ref.shape[1:]
    cols = late_cols // 2
    for y in range(NUM_Y):
        span = slice(y * part, (y + 1) * part)
        for block in range(2):
            flat_ref[span, block * cols : (block + 1) * cols] = early_ref[
                y, block * part : (block + 1) * part, :
            ]
        flat_ref[span, 2 * cols :] = late_ref[y]


def turn(early, late):
    part, late_cols = late.shape[1:]
    rhs = NUM_Y * part
    cols = late_cols // 2

    def body(early_ref, late_ref, out_ref, flat_ref):
        flatten(early_ref, late_ref, flat_ref)
        for step in range(STEPS):
            out_ref[step] = flat_ref[:, step * cols : (step + 1) * cols].T

    return pl.pallas_call(
        body,
        in_specs=[VMEM, VMEM],
        out_specs=VMEM,
        scratch_shapes=[pltpu.VMEM((rhs, STEPS * cols), BF16)],
        out_shape=pltpu.HBM((STEPS, cols, rhs), BF16),
        compiler_params=pltpu.CompilerParams(vmem_limit_bytes=SCRATCH),
        name="turn",
    )(*resident(early, late))


def product(core, factor, early, late, dtype):
    trail_rows, steps, cols = factor.shape
    depth = steps * cols
    rhs = NUM_Y * late.shape[1]
    own = trail_rows // NUM_NARROW

    def body(core_ref, factor_ref, early_ref, late_ref, out_ref, flat_ref):
        side = 1 - core_ref[0] if dtype == BF16 else core_ref[0]
        flatten(early_ref, late_ref, flat_ref)
        for half in range(NUM_CORE):

            @pl.when(side == half)
            def _():
                for i in range(NUM_X):
                    start = (NUM_CORE * i + half) * own
                    out_ref[i] = lax.dot_general(
                        factor_ref[start : start + own].reshape(own, depth),
                        flat_ref[...], ROWS_T, preferred_element_type=F32,
                    ).astype(dtype)

    return pl.pallas_call(
        body,
        in_specs=[SMEM] + [VMEM] * 3,
        out_specs=VMEM,
        scratch_shapes=[pltpu.VMEM((rhs, depth), BF16)],
        out_shape=pltpu.VMEM((NUM_X, own, rhs), dtype),
        compiler_params=pltpu.CompilerParams(vmem_limit_bytes=SCRATCH),
        name="product",
    )(core, *resident(factor, early, late))


def merge(kept, back, ahead):
    def body(kept_ref, back_ref, _, out_ref):
        for i in range(NUM_X):
            out_ref[i] = (kept_ref[i] + back_ref[i].astype(F32)).astype(BF16)

    return pl.pallas_call(
        body,
        in_specs=[VMEM, VMEM, HBM],
        out_specs=VMEM,
        out_shape=pltpu.VMEM(kept.shape, BF16),
        compiler_params=pltpu.CompilerParams(vmem_limit_bytes=SCRATCH),
        name="merge",
    )(*resident(kept, back), pltpu.with_memory_space_constraint(ahead, pltpu.HBM))


def per_device(right_side, partial_in, window_factor, inverse_t, trailing_factor):
    steps, rows, rhs = right_side.shape
    cols = inverse_t.shape[2]
    part = rhs // NUM_Y
    trail_rows = trailing_factor.shape[0]

    first = (lax.axis_index(NARROW) == 0).astype(F32)[None]
    packed, own = pack(right_side, partial_in, window_factor, inverse_t, first)
    packed = lax.all_to_all(packed, "y", 0, 0, tiled=True)
    first_terms, late_terms, inverse, window_one, window_two, window_last = unpack(
        packed, rows, part
    )

    fanned = spread(first_terms[0].astype(BF16), NARROW[::-1], NUM_NARROW)
    got = step_zero(fanned, inverse, own)
    got = lax.all_to_all(got, "z", 0, 0, tiled=True)

    solved_0, both = step_one_fan(got, first_terms, window_one, window_last)
    both = lax.all_to_all(both, NARROW[::-1], 0, 0, tiled=True)
    got = step_one(both, inverse, part, rows)
    got = total(lax.all_to_all(got, "z", 0, 0, tiled=True)).astype(BF16)

    stack = jnp.concatenate([solved_0, got, own])
    early = spread(stack, "y", NUM_Y)
    fanned = lax.all_gather(fan(late_terms, stack, window_two), NARROW, axis=0)
    share = pair(fanned, inverse, early)
    late = total(lax.all_to_all(share, "z", 0, 0, tiled=True)).astype(BF16)
    late = spread(late, "y", NUM_Y)

    core = lax.axis_index("core").astype(jnp.int32)[None]
    away = product(core, trailing_factor, early, late, BF16)
    back = lax.ppermute(away, "core", [(0, 1), (1, 0)])
    kept = product(core, trailing_factor, early, late, F32)
    solved = turn(early, late)
    kept = merge(kept, back, solved)
    trailing = total(lax.all_to_all(kept, "x", 0, 0, tiled=True))
    return (solved, trailing)


def solution(mesh):
    grid = Mesh(
        mesh.devices.reshape(NUM_Y, NUM_Z, NUM_X, NUM_CORE), ("y", "z", "x", "core")
    )
    wide = ("y", "z")
    placed = (
        P(None, wide, None),
        P(NARROW, None, wide, None),
        P(None, wide, None, NARROW),
        P(None, wide, NARROW),
        P(wide, None, NARROW),
    )
    return jax.shard_map(
        per_device,
        mesh=grid,
        in_specs=placed,
        out_specs=(P(None, NARROW, None), P(wide + NARROW, None)),
        check_vma=False,
    )
```
